256 devices in a mesh: rows: 8 (over z_hi, x), lat: 32 (over y, z_lo, core).
Axes of the slice: x: 4, y: 4, z: 8 (z_hi: 2, z_lo: 4; z = z_hi * 4 + z_lo), core: 2. Of those that a mesh axis runs over, the one named last changes fastest.
Arguments:
- residual: bfloat16 [1024, 4608], P('rows', 'lat'), may hold values from -64 to 64
- enc_weight: bfloat16 [4608, 65536], P('rows', 'lat'), may hold values from -0.09375 to 0.09375
- dec_weight: bfloat16 [65536, 4608], P('lat', 'rows'), may hold values from -0.078125 to 0.078125
- enc_bias: float32 [65536], P('lat'), may hold values from -3 to 3
- dec_bias: float32 [4608], P('rows'), may hold values from -3 to 3
- active_blocks: int32 [8, 96], replicated, may hold values from 0 to 511, as said below
- active_counts: int32 [1024], P('rows'), may hold values from 1 to 96, as said below
Outputs:
- latents: bfloat16 [1024, 65536], P('rows', 'lat')
- recon: bfloat16 [1024, 4608], P('lat', 'rows')
The draws below stay inside these ranges and needn't reach their ends.
Inputs may be any that keep to these rules, and one draw needn't show every extreme that they name: `active_blocks`: each row lists 96 different latent blocks; at most 6 of them lie among the 16 blocks of one index of lat, and exactly 6 for some index in every row. `active_counts`: in every row block some row uses all 96 entries and some row uses one.
All inputs are finite; a program needn't handle non-finite values.
Results may differ from the reference program's by a relative error of at most 0.0058.
Values may be sent and summed in bfloat16 or wider, within the bound.
No kernel may reach another device: no remote copies, remote signals or barrier semaphores. Data moves between devices by JAX's collectives and lax.ppermute only.
A program may use at most 128 MiB of HBM per device.

```python
import math
import jax
import jax.numpy as jnp

D = 4608
LAT = 65536
BLOCK = 128
CAP = 6
TOKENS = 1024
RBLOCKS = 8
SHARD_BLOCKS = 16
ACTIVE = 96
N_LAT = 32


def draw_residual(key, part):
    key_values, key_rows, key_cols = jax.random.split(key, 3)
    row_pos = jnp.arange(TOKENS, dtype=jnp.float32) / (TOKENS - 1)
    col_pos = jnp.arange(D, dtype=jnp.float32) / (D - 1)
    values = jnp.clip(jax.random.normal(key_values, (TOKENS, D), jnp.float32), -6.0, 6.0)
    row_span = math.log(10.0 / 3.0)
    row_scale = jnp.exp(jax.random.uniform(key_rows, (TOKENS,), jnp.float32) * row_span) * jnp.exp(row_pos * math.log(3.0)) / 3.0
    col_scale = jnp.exp(jax.random.uniform(key_cols, (D,), jnp.float32, math.log(0.3), 0.0)) * jnp.exp(col_pos * math.log(3.0))
    return (values * row_scale[:, None] * col_scale[None, :]).astype(jnp.bfloat16)


def draw_active_blocks(key, part):

    def draw_block(block_key):
        key_full, key_rest, key_local, key_order = jax.random.split(block_key, 4)
        full_shard = jax.random.randint(key_full, (), 0, N_LAT).astype(jnp.int32)
        others = (jnp.arange((N_LAT - 1) * CAP, dtype=jnp.int32) // CAP + full_shard + 1) % N_LAT
        others = jax.random.permutation(key_rest, others)[:ACTIVE - CAP]
        shards = jnp.concatenate([jnp.full((CAP,), full_shard, jnp.int32), others.astype(jnp.int32)])
        onehot = (shards[:, None] == jnp.arange(N_LAT, dtype=jnp.int32)[None, :]).astype(jnp.int32)
        occurrence = jnp.sum((jnp.cumsum(onehot, axis=0) - onehot) * onehot, axis=1)
        shuffles = jax.vmap(lambda shard_key: jax.random.permutation(shard_key, SHARD_BLOCKS))(jax.random.split(key_local, N_LAT))
        local_block = shuffles[shards, occurrence].astype(jnp.int32)
        block_ids = shards * SHARD_BLOCKS + local_block
        return jax.random.permutation(key_order, block_ids).astype(jnp.int32)
    return jax.vmap(draw_block)(jax.random.split(key, RBLOCKS))


def draw_active_counts(key, part):
    key_base, key_top, key_low = jax.random.split(key, 3)
    row_counts = jax.random.randint(key_base, (RBLOCKS, BLOCK), 1, ACTIVE + 1).astype(jnp.int32)
    top_row = jax.random.randint(key_top, (RBLOCKS,), 0, BLOCK).astype(jnp.int32)
    low_row = (top_row + 1 + jax.random.randint(key_low, (RBLOCKS,), 0, BLOCK - 1).astype(jnp.int32)) % BLOCK
    column = jnp.arange(BLOCK, dtype=jnp.int32)[None, :]
    row_counts = jnp.where(column == top_row[:, None], ACTIVE, row_counts)
    row_counts = jnp.where(column == low_row[:, None], 1, row_counts)
    return row_counts.reshape(TOKENS).astype(jnp.int32)


def block_levels(key, shape, pieces, least, high):
    def one(dim, parts):
        steps = jax.random.uniform(jax.random.fold_in(jax.random.fold_in(key, 6), dim), (parts,), jnp.float32, least / len(pieces), high / len(pieces))
        return jnp.repeat(jnp.exp(steps), shape[dim] // parts).reshape((-1,) + (1,) * (len(shape) - dim - 1))

    loudness = one(*pieces[0])
    for cut in pieces[1:]:
        loudness = loudness * one(*cut)
    return loudness


def noise(rng, extent, deviation, bound, pieces=(), kind=jnp.bfloat16):
    gain = block_levels(rng, extent, pieces, -0.22, 0.18) if pieces else 1.0
    values = jax.random.normal(rng, extent, jnp.float32) * deviation * gain
    return jnp.minimum(jnp.maximum(values, -bound), bound).astype(kind)


def setup_inputs(seed: int = 0) -> dict:
    key_of = jax.random.split(jax.random.key(seed), 8)
    residual = draw_residual(jax.random.fold_in(key_of[7], 71), 0)
    enc_weight = noise(key_of[1], (D, LAT), D ** -0.5, 0.09375, ((0, 8), (1, 32)))
    dec_weight = noise(key_of[2], (LAT, D), (ACTIVE * 64) ** -0.5, 0.078125, ((0, 32), (1, 8)))
    enc_bias = noise(key_of[3], (LAT,), 0.5, 3.0, ((0, 32),), jnp.float32)
    dec_bias = noise(key_of[4], (D,), 0.5, 3.0, ((0, 8),), jnp.float32)
    active_blocks = draw_active_blocks(jax.random.fold_in(key_of[7], 71), 0)
    active_counts = draw_active_counts(jax.random.fold_in(key_of[7], 71), 0)
    return dict(residual=residual, enc_weight=enc_weight, dec_weight=dec_weight, enc_bias=enc_bias, dec_bias=dec_bias, active_blocks=active_blocks, active_counts=active_counts)


def block_ranks(active_blocks):
    matches = active_blocks[:, :, None] == jnp.arange(LAT // BLOCK, dtype=jnp.int32)[None, None, :]
    slots = jnp.arange(ACTIVE, dtype=jnp.int32)[None, :, None]
    listed = jnp.any(matches, axis=1).astype(jnp.int32)
    return jnp.sum(jnp.where(matches, slots, 0), axis=1).astype(jnp.int32) + ACTIVE * (1 - listed)


def reference(residual, enc_weight, dec_weight, enc_bias, dec_bias, active_blocks, active_counts):
    wide = residual.astype(jnp.float32)
    gram_full = jnp.dot(residual.T, residual, preferred_element_type=jnp.float32)
    energy = jnp.sum(wide * wide)
    mean_sq = energy / (TOKENS * D)
    chat = (gram_full / (TOKENS * (mean_sq + 1e-5))).astype(jnp.bfloat16)
    term = jnp.dot(residual, chat, preferred_element_type=jnp.float32)
    white = (1.5 * wide - 0.5 * term).astype(jnp.bfloat16)
    pre = jnp.dot(white, enc_weight, preferred_element_type=jnp.float32) + enc_bias
    ranks = jnp.repeat(block_ranks(active_blocks), BLOCK, axis=0)
    live = (ranks < active_counts[:, None]).astype(jnp.float32)
    shaped = jnp.maximum(pre, 0.0).reshape(TOKENS, LAT // BLOCK, BLOCK) * live[:, :, None]
    latents = shaped.reshape(TOKENS, LAT).astype(jnp.bfloat16)
    recon = (jnp.dot(latents, dec_weight, preferred_element_type=jnp.float32) + dec_bias).astype(jnp.bfloat16)
    return latents, recon
```

```python
import functools

import jax
import jax.numpy as jnp
import numpy as np
from jax import lax
from jax.experimental import pallas as pl
from jax.experimental.pallas import tpu as pltpu
from jax.sharding import Mesh
from jax.sharding import PartitionSpec as P


BLOCK = 128
CAP = 6
TOKENS = 1024
D = 4608
SHARD_BLOCKS = 16
ACTIVE = 96
SLICE = 576
SUB = 32
ROWS = ("zh", "x")
LAT = ("y", "zl", "c")
SIZES = {"zh": 2, "x": 4, "y": 4, "zl": 4, "c": 2}
BF16 = jnp.bfloat16
F32 = jnp.float32

VMEM = pl.BlockSpec(memory_space=pltpu.VMEM)
SMEM = pl.BlockSpec(memory_space=pltpu.SMEM)


def swap(value, axis, k):
    return lax.ppermute(value, axis, [(i, i ^ k) for i in range(SIZES[axis])])


def gather4(value, axis):
    far, near, last = (swap(value, axis, k) for k in (2, 1, 3))
    return jnp.concatenate([value, near, far, last], axis=0)


def call(kernel, outs, operands, specs, name, flops=0, size=0):
    return pl.pallas_call(
        kernel,
        out_shape=outs,
        in_specs=specs,
        out_specs=jax.tree.map(lambda _: VMEM, outs),
        name=name,
        cost_estimate=pl.CostEstimate(flops=flops, bytes_accessed=size, transcendentals=0),
    )(*operands)


def bits(pos):
    return pos[0], pos[1], pos[2], pos[3], pos[4]


def gram_kernel(pos, near, other, counts, wide, narrow):
    zh, x, y, zl, c = bits(pos)
    own = near[0:SUB, :]
    dims = (((1,), (1,)), ((), ()))
    total = jnp.zeros((1, 1), F32)
    for part, half in enumerate((near, other)):
        value = half[...]
        g = lax.dot_general(own, value, dims, preferred_element_type=F32)
        wide[:, part * 512 : (part + 1) * 512] = g
        narrow[:, part * 512 : (part + 1) * 512] = g.astype(BF16)
        spread = value.astype(F32)
        total = total + jnp.sum(jnp.sum(spread * spread, axis=0, keepdims=True), axis=1, keepdims=True)
    total = jnp.broadcast_to(total, (SUB, BLOCK))
    high = total.astype(BF16).astype(F32)
    mid = (total - high).astype(BF16).astype(F32)
    low = (total - high - mid).astype(BF16).astype(F32)
    row = lax.broadcasted_iota(jnp.int32, (SUB, BLOCK), 0)
    extra = jnp.where(row == zh * 4 + x, jnp.broadcast_to(counts[...], (SUB, BLOCK)), 0.0)
    extra = jnp.where(row == 8, high, jnp.where(row == 9, mid, jnp.where(row == 10, low, extra)))
    wide[:, TOKENS:] = extra
    narrow[:, TOKENS:] = extra.astype(BF16)


def white_kernel(mine, theirs, near, other, out):
    g = mine[...] + theirs[...]
    extra = g[:, TOKENS:]
    energy = extra[8:9, 0:1] + extra[9:10, 0:1] + extra[10:11, 0:1]
    mean_sq = energy / (TOKENS * D)
    scale = 1.0 / (TOKENS * (mean_sq + 1e-05))
    chat = g[:, :TOKENS] * scale
    high = chat.astype(BF16)
    low = (chat - high.astype(F32)).astype(BF16)
    both = jnp.concatenate([high, low], axis=0)
    term = jnp.dot(both[:, :512], near[...], preferred_element_type=F32)
    term = term + jnp.dot(both[:, 512:], other[...], preferred_element_type=F32)
    own = near[0:SUB, :].astype(F32)
    out[...] = (1.5 * own - 0.5 * (term[:SUB] + term[SUB:])).astype(BF16)


def encode_kernel(pos, tab, near, other, weight, o0, o1, o2, o3):
    zh, x, y, zl, c = bits(pos)
    for k, out in enumerate((o0, o1, o2, o3)):
        xb = x ^ k
        jy = y ^ xb
        for jc, half in enumerate((near, other)):
            zb = c ^ jc
            b = zb * 4 + xb
            rows = jnp.concatenate(
                [half[pl.ds(pl.multiple_of(jy * BLOCK + (zl ^ q) * SUB, SUB), SUB), :] for q in range(4)], axis=0
            )
            for p in range(CAP // 2):
                cols = [
                    weight[:, pl.ds(pl.multiple_of(tab[b, 2 * p + e] * BLOCK, BLOCK), BLOCK)] for e in range(2)
                ]
                part = jnp.dot(rows, jnp.concatenate(cols, axis=1), preferred_element_type=F32)
                out[zb, :, 2 * p * BLOCK : (2 * p + 2) * BLOCK] = part.astype(BF16)


def latent_kernel(pos, tab, mine, theirs, bias, counts, out):
    zh, x, y, zl, c = bits(pos)
    for zb in range(2):
        b = zb * 4 + x
        for s in range(CAP):
            cols = slice(s * BLOCK, (s + 1) * BLOCK)
            pre = mine[zb, :, cols] + theirs[zb, :, cols].astype(F32) + bias[pl.ds(tab[b, s], 1), :]
            rank = tab[b, 8 + s].astype(F32)
            out[zb, :, cols] = jnp.where(rank < counts[zb], jnp.maximum(pre, 0.0), 0.0).astype(BF16)


def spread_kernel(pos, tab, lat, out):
    zh, x, y, zl, c = bits(pos)
    out[...] = jnp.zeros_like(out)
    b = zh * 4 + x
    for s in range(CAP):
        @pl.when(tab[b, 8 + s] < ACTIVE)
        def _():
            start = pl.multiple_of(tab[b, s] * BLOCK, BLOCK)
            out[:, pl.ds(start, BLOCK)] = lat[zh, :, s * BLOCK : (s + 1) * BLOCK]


def decode_kernel(pos, tab, l0, l1, l2, l3, weight, mine, theirs):
    zh, x, y, zl, c = bits(pos)
    for k, lat in enumerate((l0, l1, l2, l3)):
        xb = x ^ k
        for zb in range(2):
            b = zb * 4 + xb
            starts = [q * 64 + e * SUB for e in (c, 1 - c) for q in range(2)]
            rows = jnp.concatenate([lat[zb, pl.ds(pl.multiple_of(s, SUB), SUB), :] for s in starts], axis=0)
            acc = jnp.zeros((BLOCK, SLICE), F32)
            for p in range(CAP // 2):
                tiles = [
                    weight[pl.ds(pl.multiple_of(tab[b, 2 * p + e] * BLOCK, BLOCK), BLOCK), :] for e in range(2)
                ]
                acc = acc + jnp.dot(
                    rows[:, 2 * p * BLOCK : (2 * p + 2) * BLOCK],
                    jnp.concatenate(tiles, axis=0),
                    preferred_element_type=F32,
                )
            ky = (zb * 2 + xb // 2) ^ y
            first = (2 * (xb & 1)) ^ zl
            for q in range(2):
                kz = first ^ q
                mine[ky, kz] = acc[q * SUB : (q + 1) * SUB]
                theirs[ky, kz] = acc[64 + q * SUB : 64 + (q + 1) * SUB].astype(BF16)


def tables(active_blocks, lat_index):
    ids = lat_index * SHARD_BLOCKS + jnp.arange(SHARD_BLOCKS, dtype=jnp.int32)
    matches = active_blocks[:, :, None] == ids[None, None, :]
    places = jnp.arange(ACTIVE, dtype=jnp.int32)[None, :, None]
    rank = jnp.sum(jnp.where(matches, places, 0), axis=1)
    listed = jnp.any(matches, axis=1).astype(jnp.int32)
    block = jnp.arange(SHARD_BLOCKS, dtype=jnp.int32)
    before = (block[:, None] < block[None, :]).astype(jnp.int32)
    slot = jnp.sum(listed[:, :, None] * before[None], axis=1)
    chosen = (slot[:, :, None] == jnp.arange(8, dtype=jnp.int32)[None, None, :]) & (listed[:, :, None] > 0)
    index = jnp.sum(jnp.where(chosen, block[None, :, None], 0), axis=1)
    ranks = jnp.sum(jnp.where(chosen, rank[:, :, None] - ACTIVE, 0), axis=1) + ACTIVE
    return jnp.concatenate([index, ranks], axis=1)


def shards(residual, enc_weight, dec_weight, enc_bias, dec_bias, active_blocks, active_counts):
    zh, x, y, zl, c = (lax.axis_index(a) for a in ("zh", "x", "y", "zl", "c"))
    pos = jnp.stack([zh, x, y, zl, c]).astype(jnp.int32)
    tab = tables(active_blocks, (y * 4 + zl) * 2 + c)

    group = (zl & 1) * 2 + c
    pieces = []
    for k in range(4):
        pairs = []
        for source in range(256):
            r, lat = divmod(source, 32)
            j = (lat & 3) ^ k
            pairs.append((source, (lat // 4) * 32 + (r & 3) * 8 + j * 2 + r // 4))
        piece = lax.dynamic_slice_in_dim(residual, (group ^ k) * SUB, SUB, 0)
        pieces.append(lax.ppermute(piece, ROWS + LAT, pairs))
    pieces = jnp.stack(pieces)
    own = jnp.concatenate(
        [lax.dynamic_index_in_dim(pieces, zl ^ m, 0, keepdims=False) for m in range(4)], axis=1
    )
    near = gather4(gather4(own, "zl"), "y")
    other = swap(near, "c", 1)

    counts = active_counts.astype(F32).reshape(1, BLOCK)
    wide, narrow = call(
        gram_kernel,
        (jax.ShapeDtypeStruct((SUB, TOKENS + BLOCK), F32), jax.ShapeDtypeStruct((SUB, TOKENS + BLOCK), BF16)),
        (pos, near, other, counts),
        [SMEM, VMEM, VMEM, VMEM],
        "gram",
        flops=2 * SUB * TOKENS * SLICE,
        size=1500000,
    )
    far, by1, by3 = (swap(narrow, "x", k) for k in (2, 1, 3))
    mine = wide + by1.astype(F32) + far.astype(F32) + by3.astype(F32)
    theirs = swap(mine, "zh", 1)
    white = call(
        white_kernel,
        jax.ShapeDtypeStruct((SUB, SLICE), BF16),
        (mine, theirs, near, other),
        [VMEM] * 4,
        "white",
        flops=4 * SUB * TOKENS * SLICE,
        size=1500000,
    )
    every = (mine + theirs)[:8, TOKENS:]
    row_counts = jnp.stack([lax.dynamic_index_in_dim(every, 4 * zb + x, 0, keepdims=False) for zb in range(2)])
    row_counts = jnp.broadcast_to(row_counts[:, :, None], (2, BLOCK, BLOCK))

    white_near = gather4(gather4(white, "zl"), "y")
    white_other = swap(white_near, "c", 1)
    wide_piece = jax.ShapeDtypeStruct((2, BLOCK, CAP * BLOCK), BF16)
    p0, p1, p2, p3 = call(
        encode_kernel,
        (wide_piece,) * 4,
        (pos, tab, white_near, white_other, enc_weight),
        [SMEM, SMEM, VMEM, VMEM, VMEM],
        "encode",
        flops=2 * TOKENS * SLICE * CAP * BLOCK,
        size=5000000,
    )
    q2, q1, q3 = swap(p2, "x", 2), swap(p1, "x", 1), swap(p3, "x", 3)
    mine = p0.astype(F32) + q1.astype(F32) + q2.astype(F32) + q3.astype(F32)
    theirs = swap(mine.astype(BF16), "zh", 1)
    lat = call(
        latent_kernel,
        wide_piece,
        (pos, tab, mine, theirs, enc_bias.reshape(SHARD_BLOCKS, BLOCK), row_counts),
        [SMEM, SMEM, VMEM, VMEM, VMEM, VMEM],
        "latent",
        size=1500000,
    )
    lat2, lat1, lat3 = (swap(lat, "x", k) for k in (2, 1, 3))
    latents = call(
        spread_kernel,
        jax.ShapeDtypeStruct((BLOCK, SHARD_BLOCKS * BLOCK), BF16),
        (pos, tab, lat),
        [SMEM, SMEM, VMEM],
        "spread",
        size=1000000,
    )
    mine, theirs = call(
        decode_kernel,
        (jax.ShapeDtypeStruct((4, 4, SUB, SLICE), F32), jax.ShapeDtypeStruct((4, 4, SUB, SLICE), BF16)),
        (pos, tab, lat, lat1, lat2, lat3, dec_weight),
        [SMEM, SMEM] + [VMEM] * 5,
        "decode",
        flops=2 * TOKENS * SLICE * CAP * BLOCK,
        size=7000000,
    )
    mine = mine + swap(theirs, "c", 1).astype(F32)
    sent = mine.astype(BF16)
    r2, r1, r3 = (swap(sent[k], "y", k) for k in (2, 1, 3))
    mine = mine[0] + r1.astype(F32) + r2.astype(F32) + r3.astype(F32)
    sent = mine.astype(BF16)
    r2, r1, r3 = (swap(sent[k], "zl", k) for k in (2, 1, 3))
    recon = mine[0] + r1.astype(F32) + r2.astype(F32) + r3.astype(F32)
    recon = (recon + dec_bias).astype(BF16)
    return latents, recon


def solution(mesh):
    fine = Mesh(mesh.devices.reshape(tuple(SIZES.values())), tuple(SIZES))
    in_specs = (P(ROWS, LAT), P(ROWS, LAT), P(LAT, ROWS), P(LAT), P(ROWS), P(), P(ROWS))
    out_specs = (P(ROWS, LAT), P(LAT, ROWS))
    return jax.shard_map(shards, mesh=fine, in_specs=in_specs, out_specs=out_specs, check_vma=False)
```

```python
import functools

import jax
import jax.numpy as jnp
import numpy as np
from jax import lax
from jax.experimental import pallas as pl
from jax.experimental.pallas import tpu as pltpu
from jax.sharding import Mesh
from jax.sharding import PartitionSpec as P


BLOCK = 128
CAP = 6
TOKENS = 1024
D = 4608
SHARD_BLOCKS = 16
ACTIVE = 96
SLICE = 576
SUB = 32
ROWS = ("zh", "x")
LAT = ("y", "zl", "c")
SIZES = {"zh": 2, "x": 4, "y": 4, "zl": 4, "c": 2}
BF16 = jnp.bfloat16
F32 = jnp.float32

VMEM = pl.BlockSpec(memory_space=pltpu.VMEM)
SMEM = pl.BlockSpec(memory_space=pltpu.SMEM)
ANY = pl.BlockSpec(memory_space=pl.ANY)


def swap(value, axis, k):
    return lax.ppermute(value, axis, [(i, i ^ k) for i in range(SIZES[axis])])


def gather4(value, axis):
    far, near, last = (swap(value, axis, k) for k in (2, 1, 3))
    return jnp.concatenate([value, near, far, last], axis=0)


def call(kernel, outs, operands, specs, name, flops=0, size=0, scratch=()):
    return pl.pallas_call(
        kernel,
        out_shape=outs,
        in_specs=specs,
        out_specs=jax.tree.map(lambda _: VMEM, outs),
        name=name,
        scratch_shapes=scratch,
        compiler_params=pltpu.CompilerParams(vmem_limit_bytes=GRANT),
        cost_estimate=pl.CostEstimate(flops=flops, bytes_accessed=size, transcendentals=0),
    )(*operands)


def bits(pos):
    return pos[0], pos[1], pos[2], pos[3], pos[4]


GRANT = 10 * 2**20
WIDE = TOKENS + 2 * BLOCK


def on_diagonal(y, zl, c):
    shape = (SUB, TOKENS)
    row = lax.broadcasted_iota(jnp.int32, shape, 0)
    return lax.broadcasted_iota(jnp.int32, shape, 1) == row + ((y * 4 + zl) * 2 + c) * SUB


def split3(value):
    high = value.astype(BF16).astype(F32)
    mid = (value - high).astype(BF16).astype(F32)
    return high, mid, (value - high - mid).astype(BF16).astype(F32)


def gram_kernel(pos, near, other, counts, wide, narrow, full, own):
    zh, x, y, zl, c = bits(pos)
    for jc, half in enumerate((near, other)):
        for jy in range(4):
            for jz in range(4):
                zs = zl ^ jz
                feature = pl.multiple_of(((zs & 1) * 2 + (c ^ jc)) * 144, 16)
                row = pl.multiple_of(((y ^ jy) * 2 + zs // 2) * BLOCK, BLOCK)
                full[pl.ds(feature, 144), pl.ds(row, BLOCK)] = half[jy * 4 + jz]
    rows = full[:, pl.ds(pl.multiple_of((y * 2 + zl // 2) * BLOCK, BLOCK), BLOCK)].astype(F32).T.astype(BF16)
    group = (zl & 1) * 2 + c
    mine = rows[0:SUB]
    for g in range(1, 4):
        mine = jnp.where(group == g, rows[g * SUB : (g + 1) * SUB], mine)
    own[...] = mine
    g = jnp.dot(mine, full[...], preferred_element_type=F32)
    mask = on_diagonal(y, zl, c)
    diagonal = jnp.sum(jnp.where(mask, g, 0.0), axis=1, keepdims=True)
    g = jnp.where(mask, 0.0, g)
    wide[:, :TOKENS] = g
    narrow[:, :TOKENS] = g.astype(BF16)
    spread = full[...].astype(F32)
    total = jnp.sum(jnp.sum(spread * spread, axis=0, keepdims=True), axis=1, keepdims=True)
    shape = (SUB, BLOCK)
    row = lax.broadcasted_iota(jnp.int32, shape, 0)
    lane = lax.broadcasted_iota(jnp.int32, shape, 1)
    extra = jnp.where(row == zh * 4 + x, jnp.broadcast_to(counts[...], shape), 0.0)
    wide[:, TOKENS : TOKENS + BLOCK] = extra
    narrow[:, TOKENS : TOKENS + BLOCK] = extra.astype(BF16)
    extra = jnp.zeros(shape, F32)
    columns = split3(jnp.broadcast_to(diagonal, shape)) + split3(jnp.broadcast_to(total, shape))
    for i, column in enumerate(columns):
        extra = jnp.where(lane == i, column, extra)
    wide[:, TOKENS + BLOCK :] = extra
    narrow[:, TOKENS + BLOCK :] = extra.astype(BF16)


def white_kernel(pos, mine, theirs, full, own, out):
    zh, x, y, zl, c = bits(pos)
    g = mine[...] + theirs[...]
    extra = g[:, TOKENS + BLOCK :]
    diagonal = extra[:, 0:1] + extra[:, 1:2] + extra[:, 2:3]
    energy = extra[:, 3:4] + extra[:, 4:5] + extra[:, 5:6]
    mean_sq = energy / (TOKENS * D)
    g = jnp.where(on_diagonal(y, zl, c), diagonal, g[:, :TOKENS])
    chat = g / (TOKENS * (mean_sq + 1e-05))
    high = chat.astype(BF16)
    low = (chat - high.astype(F32)).astype(BF16)
    both = jnp.concatenate([high, low], axis=0)
    term = lax.dot_general(both, full[...], (((1,), (1,)), ((), ())), preferred_element_type=F32)
    out[0] = (1.5 * own[...].astype(F32) - 0.5 * (term[:SUB] + term[SUB:])).astype(BF16)


def counts_kernel(pos, mine, theirs, out, tile):
    tile[...] = mine[0:8, TOKENS : TOKENS + BLOCK] + theirs[0:8, TOKENS : TOKENS + BLOCK]
    for zb in range(2):
        row = tile[pl.ds(pos[1] + 4 * zb, 1), :]
        out[zb] = jnp.broadcast_to(row, (BLOCK, BLOCK)).T


def encode_kernel(pos, tab, after, half, weight, o0, o1, o2, o3):
    zh, x, y, zl, c = bits(pos)
    for k, out in ((2, o2), (1, o1), (3, o3), (0, o0)):
        xb = x ^ k
        for zb in range(2):
            b = zb * 4 + xb
            jy = y ^ (zb * 2 + xb // 2)
            rows = jnp.concatenate([half[jy * 4 + (zl ^ ((xb & 1) * 2 + q))] for q in range(2)], axis=0)
            for p in range(CAP // 2):
                cols = [
                    weight[:, pl.ds(pl.multiple_of(tab[b, 2 * p + e] * BLOCK, BLOCK), BLOCK)] for e in range(2)
                ]
                part = jnp.dot(rows, jnp.concatenate(cols, axis=1), preferred_element_type=F32)
                out[zb, :, 2 * p * BLOCK : (2 * p + 2) * BLOCK] = part.astype(BF16)


def sum_kernel(after, p0, p1, p2, p3, wide, narrow):
    total = p0[...].astype(F32) + p1[...].astype(F32) + p2[...].astype(F32) + p3[...].astype(F32)
    wide[...] = total
    narrow[...] = total.astype(BF16)


def latent_kernel(jc, pos, tab, after, mine, theirs, bias, counts, out):
    zh, x, y, zl, c = bits(pos)
    for zb in range(2):
        b = zb * 4 + x
        starts = [pl.multiple_of(q * 64 + (c ^ jc) * SUB, SUB) for q in range(2)]
        limits = jnp.concatenate([counts[zb, pl.ds(start, SUB), :] for start in starts], axis=0)
        for s in range(CAP):
            cols = slice(s * BLOCK, (s + 1) * BLOCK)
            pre = mine[zb, :, cols] + theirs[zb, :, cols].astype(F32) + bias[pl.ds(tab[b, s], 1), :]
            rank = tab[b, 8 + s].astype(F32)
            out[zb, :, cols] = jnp.where(rank < limits, jnp.maximum(pre, 0.0), 0.0).astype(BF16)


def spread_kernel(pos, tab, near, other, out):
    zh, x, y, zl, c = bits(pos)
    out[...] = jnp.zeros_like(out)
    b = zh * 4 + x
    for s in range(CAP):
        @pl.when(tab[b, 8 + s] < ACTIVE)
        def _():
            start = pl.multiple_of(tab[b, s] * BLOCK, BLOCK)
            for jc, lat in enumerate((near, other)):
                for q in range(2):
                    row = pl.multiple_of(q * 64 + (c ^ jc) * SUB, SUB)
                    value = lat[zh, q * SUB : (q + 1) * SUB, s * BLOCK : (s + 1) * BLOCK]
                    out[pl.ds(row, SUB), pl.ds(start, BLOCK)] = value


def decode_kernel(pos, tab, after, l0, l1, l2, l3, weight, out):
    zh, x, y, zl, c = bits(pos)
    for k, lat in enumerate((l0, l1, l2, l3)):
        xb = x ^ k
        for zb in range(2):
            b = zb * 4 + xb
            acc = jnp.zeros((2 * SUB, SLICE), F32)
            for p in range(CAP // 2):
                tiles = [
                    weight[:, pl.ds(pl.multiple_of(tab[b, 2 * p + e] * BLOCK, BLOCK), BLOCK)] for e in range(2)
                ]
                acc = acc + lax.dot_general(
                    lat[zb, :, 2 * p * BLOCK : (2 * p + 2) * BLOCK],
                    jnp.concatenate(tiles, axis=1),
                    (((1,), (1,)), ((), ())),
                    preferred_element_type=F32,
                )
            ky = (zb * 2 + xb // 2) ^ y
            for q in range(2):
                out[ky, ((xb & 1) * 2 + q) ^ zl] = acc[q * SUB : (q + 1) * SUB].astype(out.dtype)


def tables(active_blocks, lat_index):
    ids = lat_index * SHARD_BLOCKS + jnp.arange(SHARD_BLOCKS, dtype=jnp.int32)
    matches = active_blocks[:, :, None] == ids[None, None, :]
    places = jnp.arange(ACTIVE, dtype=jnp.int32)[None, :, None]
    rank = jnp.sum(jnp.where(matches, places, 0), axis=1)
    listed = jnp.any(matches, axis=1).astype(jnp.int32)
    block = jnp.arange(SHARD_BLOCKS, dtype=jnp.int32)
    before = (block[:, None] < block[None, :]).astype(jnp.int32)
    slot = jnp.sum(listed[:, :, None] * before[None], axis=1)
    chosen = (slot[:, :, None] == jnp.arange(8, dtype=jnp.int32)[None, None, :]) & (listed[:, :, None] > 0)
    index = jnp.sum(jnp.where(chosen, block[None, :, None], 0), axis=1)
    ranks = jnp.sum(jnp.where(chosen, rank[:, :, None] - ACTIVE, 0), axis=1) + ACTIVE
    return jnp.concatenate([index, ranks], axis=1)


def shards(residual, enc_weight, dec_weight, enc_bias, dec_bias, active_blocks, active_counts):
    zh, x, y, zl, c = (lax.axis_index(a) for a in ("zh", "x", "y", "zl", "c"))
    pos = jnp.stack([zh, x, y, zl, c]).astype(jnp.int32)
    tab = tables(active_blocks, (y * 4 + zl) * 2 + c)

    pairs = []
    for source in range(256):
        r, lat = divmod(source, 32)
        pairs.append((source, (lat // 4) * 32 + r * 4 + lat % 4))
    own = lax.ppermute(residual.T, ROWS + LAT, pairs)
    near = gather4(gather4(own[None], "zl"), "y")
    other = swap(near, "c", 1)

    counts = active_counts.astype(F32).reshape(1, BLOCK)
    wide, narrow, full, own = call(
        gram_kernel,
        (
            jax.ShapeDtypeStruct((SUB, WIDE), F32),
            jax.ShapeDtypeStruct((SUB, WIDE), BF16),
            jax.ShapeDtypeStruct((SLICE, TOKENS), BF16),
            jax.ShapeDtypeStruct((SUB, SLICE), BF16),
        ),
        (pos, near, other, counts),
        [SMEM, VMEM, VMEM, VMEM],
        "gram",
        flops=2 * SUB * TOKENS * SLICE,
        size=1500000,
    )
    far, by1, by3 = (swap(narrow, "x", k) for k in (2, 1, 3))
    mine = wide + by1.astype(F32) + far.astype(F32) + by3.astype(F32)
    theirs = swap(mine, "zh", 1)
    white = call(
        white_kernel,
        jax.ShapeDtypeStruct((1, SUB, SLICE), BF16),
        (pos, mine, theirs, full, own),
        [SMEM] + [VMEM] * 4,
        "white",
        flops=4 * SUB * TOKENS * SLICE,
        size=1500000,
    )
    counts = call(
        counts_kernel,
        jax.ShapeDtypeStruct((2, BLOCK, BLOCK), F32),
        (pos, mine, theirs),
        [SMEM, VMEM, VMEM],
        "counts",
        size=500000,
        scratch=[pltpu.VMEM((8, BLOCK), F32)],
    )

    white_near = gather4(gather4(white, "zl"), "y")
    white_other = swap(white_near, "c", 1)
    bias = enc_bias.reshape(SHARD_BLOCKS, BLOCK)
    piece = jax.ShapeDtypeStruct((2, 2 * SUB, CAP * BLOCK), BF16)
    halves = (white_near, white_other)
    chunks = range(2)
    sent, mine, sums, lats, outs = [], [], [], [], []
    for jc in chunks:
        sent.append(
            call(
                encode_kernel,
                (piece,) * 4,
                (pos, tab, sent[0][0] if jc else white_near, halves[jc], enc_weight),
                [SMEM, SMEM, ANY, VMEM, VMEM],
                "encode",
                flops=TOKENS * SLICE * CAP * BLOCK,
                size=4000000,
            )
        )
    arrived = [[swap(sent[jc][k], "x", k) for k in (2, 1, 3)] for jc in chunks]
    for jc in chunks:
        sums.append(
            call(
                sum_kernel,
                (jax.ShapeDtypeStruct(piece.shape, F32), piece),
                (sums[0][1] if jc else white_near, sent[jc][0], *arrived[jc]),
                [ANY] + [VMEM] * 4,
                "sum",
                size=1400000,
            )
        )
    theirs = [swap(sums[jc][1], "zh", 1) for jc in chunks]
    for jc in chunks:
        lats.append(
            call(
                functools.partial(latent_kernel, jc),
                piece,
                (pos, tab, lats[0] if jc else white_near, sums[jc][0], theirs[jc], bias, counts),
                [SMEM, SMEM, ANY, VMEM, VMEM, VMEM, VMEM],
                "latent",
                size=1000000,
            )
        )
    arrived = [[swap(lats[jc], "x", k) for k in (2, 1, 3)] for jc in chunks]
    for jc in chunks:
        far, by1, by3 = arrived[jc]
        outs.append(
            call(
                decode_kernel,
                jax.ShapeDtypeStruct((4, 4, SUB, SLICE), BF16 if jc else F32),
                (pos, tab, outs[0] if jc else white_near, lats[jc], by1, far, by3, dec_weight.T),
                [SMEM, SMEM, ANY] + [VMEM] * 5,
                "decode",
                flops=TOKENS * SLICE * CAP * BLOCK,
                size=5000000,
            )
        )
    latents = call(
        spread_kernel,
        jax.ShapeDtypeStruct((BLOCK, SHARD_BLOCKS * BLOCK), BF16),
        (pos, tab, *lats),
        [SMEM, SMEM, VMEM, VMEM],
        "spread",
        size=1000000,
    )
    mine = outs[0] + swap(outs[1], "c", 1).astype(F32)
    sent = mine.astype(BF16)
    r2, r1, r3 = (swap(sent[k], "y", k) for k in (2, 1, 3))
    mine = mine[0] + r1.astype(F32) + r2.astype(F32) + r3.astype(F32)
    sent = mine.astype(BF16)
    r2, r1, r3 = (swap(sent[k], "zl", k) for k in (2, 1, 3))
    recon = mine[0] + r1.astype(F32) + r2.astype(F32) + r3.astype(F32)
    recon = (recon + dec_bias).astype(BF16)
    return latents, recon


def solution(mesh):
    fine = Mesh(mesh.devices.reshape(tuple(SIZES.values())), tuple(SIZES))
    in_specs = (P(ROWS, LAT), P(ROWS, LAT), P(LAT, ROWS), P(LAT), P(ROWS), P(), P(ROWS))
    out_specs = (P(ROWS, LAT), P(LAT, ROWS))
    return jax.shard_map(shards, mesh=fine, in_specs=in_specs, out_specs=out_specs, check_vma=False)
```

```python
import functools

import jax
import jax.numpy as jnp
from jax import lax
from jax.experimental import pallas as pl
from jax.experimental.pallas import tpu as pltpu
from jax.sharding import Mesh
from jax.sharding import PartitionSpec as P


BLOCK = 128
CAP = 6
TOKENS = 1024
D = 4608
SHARD_BLOCKS = 16
ACTIVE = 96
SLICE = 576
SUB = 32
ROWS = ("zh", "x")
LAT = ("y", "zl", "c")
SIZES = {"zh": 2, "x": 4, "y": 4, "zl": 4, "c": 2}
BF16 = jnp.bfloat16
F32 = jnp.float32

VMEM = pl.BlockSpec(memory_space=pltpu.VMEM)
SMEM = pl.BlockSpec(memory_space=pltpu.SMEM)
ANY = pl.BlockSpec(memory_space=pl.ANY)


def swap(value, axis, k):
    return lax.ppermute(value, axis, [(i, i ^ k) for i in range(SIZES[axis])])


def gather4(value, axis):
    far, near, last = (swap(value, axis, k) for k in (2, 1, 3))
    return jnp.concatenate([value, near, far, last], axis=0)


def call(kernel, outs, operands, specs, flops=0, size=0, scratch=()):
    return pl.pallas_call(
        kernel,
        out_shape=outs,
        in_specs=specs,
        out_specs=jax.tree.map(lambda _: VMEM, outs),
        scratch_shapes=scratch,
        compiler_params=pltpu.CompilerParams(vmem_limit_bytes=GRANT),
        cost_estimate=pl.CostEstimate(flops=flops, bytes_accessed=size, transcendentals=0),
    )(*operands)


def bits(pos):
    return pos[0], pos[1], pos[2], pos[3], pos[4]


GRANT = 10 * 2**20
WIDE = TOKENS + BLOCK


def row_group(zh, y, zl, c):
    return (y * 4 + (zl ^ (3 * zh))) * 2 + c


def on_diagonal(group):
    shape = (SUB, TOKENS)
    row = lax.broadcasted_iota(jnp.int32, shape, 0)
    return lax.broadcasted_iota(jnp.int32, shape, 1) == row + group * SUB


def split3(value):
    high = value.astype(BF16).astype(F32)
    mid = (value - high).astype(BF16).astype(F32)
    return high, mid, (value - high - mid).astype(BF16).astype(F32)


def pack(counts, diagonal, energy):
    row = lax.broadcasted_iota(jnp.int32, (SUB, BLOCK), 0)
    extra = jnp.where(row < 8, counts, 0.0)
    for i, part in enumerate(split3(diagonal) + split3(energy)):
        extra = jnp.where(row == 8 + i, part, extra)
    return extra


def gram_kernel(pos, near, other, counts, wide, narrow, full, own):
    zh, x, y, zl, c = bits(pos)
    for jc, half in enumerate((near, other)):
        for jy in range(4):
            for jz in range(4):
                zs = zl ^ jz
                feature = pl.multiple_of(((zs & 1) * 2 + (c ^ jc)) * 144, 16)
                row = pl.multiple_of(((y ^ jy) * 2 + zs // 2) * BLOCK, BLOCK)
                full[pl.ds(feature, 144), pl.ds(row, BLOCK)] = half[jy * 4 + jz]
    group = row_group(zh, y, zl, c)
    rows = full[:, pl.ds(pl.multiple_of(group // 4 * BLOCK, BLOCK), BLOCK)].astype(F32).T.astype(BF16)
    mine = rows[0:SUB]
    for g in range(1, 4):
        mine = jnp.where(group % 4 == g, rows[g * SUB : (g + 1) * SUB], mine)
    own[...] = mine
    g = jnp.dot(mine, full[...], preferred_element_type=F32)
    mask = on_diagonal(group)
    diagonal = jnp.sum(jnp.where(mask, g, 0.0), axis=0, keepdims=True)
    diagonal = sum(diagonal[:, i * BLOCK : (i + 1) * BLOCK] for i in range(TOKENS // BLOCK))
    g = jnp.where(mask, 0.0, g)
    wide[:, :TOKENS] = g
    narrow[:, :TOKENS] = g.astype(BF16)
    spread = full[...].astype(F32)
    total = jnp.sum(jnp.sum(spread * spread, axis=0, keepdims=True), axis=1, keepdims=True)
    shape = (SUB, BLOCK)
    row = lax.broadcasted_iota(jnp.int32, shape, 0)
    spot = jnp.where(row == zh * 4 + x, jnp.broadcast_to(counts[...], shape), 0.0)
    extra = pack(spot, jnp.broadcast_to(diagonal, shape), jnp.broadcast_to(total, shape))
    wide[:, TOKENS:] = extra
    narrow[:, TOKENS:] = extra.astype(BF16)


def unpack(extra):
    return extra[8:9] + extra[9:10] + extra[10:11], extra[11:12] + extra[12:13] + extra[13:14]


def gram_sum_kernel(mine, by1, by2, by3, wide, narrow):
    g = mine[...] + by1[...].astype(F32) + by2[...].astype(F32) + by3[...].astype(F32)
    wide[...] = g
    narrow[:, :TOKENS] = g[:, :TOKENS].astype(BF16)
    extra = g[:, TOKENS:]
    shape = (SUB, BLOCK)
    diagonal, energy = (jnp.broadcast_to(v, shape) for v in unpack(extra))
    narrow[:, TOKENS:] = pack(extra, diagonal, energy).astype(BF16)


def white_kernel(pos, mine, theirs, full, own, out):
    zh, _, y, zl, c = bits(pos)
    g = mine[...] + theirs[...].astype(F32)
    diagonal, energy = unpack(g[:, TOKENS:])
    mean_sq = energy[:, 0:1] / (TOKENS * D)
    diagonal = jnp.broadcast_to(jnp.concatenate([diagonal] * (TOKENS // BLOCK), axis=1), (SUB, TOKENS))
    g = jnp.where(on_diagonal(row_group(zh, y, zl, c)), diagonal, g[:, :TOKENS])
    chat = g / (TOKENS * (mean_sq + 1e-05))
    high = chat.astype(BF16)
    low = (chat - high.astype(F32)).astype(BF16)
    both = jnp.concatenate([high, low], axis=0)
    term = lax.dot_general(both, full[...], (((1,), (1,)), ((), ())), preferred_element_type=F32)
    out[0] = (1.5 * own[...].astype(F32) - 0.5 * (term[:SUB] + term[SUB:])).astype(BF16)


def counts_kernel(pos, mine, theirs, out, tile):
    tile[...] = mine[0:8, TOKENS:] + theirs[0:16, TOKENS:].astype(F32)[0:8]
    for zb in range(2):
        row = tile[pl.ds(pos[1] + 4 * zb, 1), :]
        out[zb] = jnp.broadcast_to(row, (BLOCK, BLOCK)).T


def encode_kernel(h, pos, tab, after, near, other, weight, o0, o1, o2, o3):
    zh, x, y, zl, _ = bits(pos)
    for k, out in ((2, o2), (1, o1), (3, o3), (0, o0)):
        xb = x ^ k
        for zb in range(2):
            b = zb * 4 + xb
            jy = y ^ (zb * 2 + xb // 2)
            place = jy * 4 + (zl ^ (3 * zh) ^ ((xb & 1) * 2 + h))
            rows = jnp.concatenate([near[place], other[place]], axis=0)
            for p in range(CAP // 2):
                cols = [
                    weight[:, pl.ds(pl.multiple_of(tab[b, 2 * p + e] * BLOCK, BLOCK), BLOCK)] for e in range(2)
                ]
                part = jnp.dot(rows, jnp.concatenate(cols, axis=1), preferred_element_type=F32)
                out[zb, :, 2 * p * BLOCK : (2 * p + 2) * BLOCK] = part.astype(BF16)


def sum_kernel(after, p0, p1, p2, p3, wide, narrow):
    total = p0[...].astype(F32) + p1[...].astype(F32) + p2[...].astype(F32) + p3[...].astype(F32)
    wide[...] = total
    narrow[...] = total.astype(BF16)


def latent_kernel(h, pos, tab, after, mine, theirs, bias, counts, out):
    _, x, _, _, c = bits(pos)
    for zb in range(2):
        b = zb * 4 + x
        starts = [pl.multiple_of(h * 64 + (c ^ jc) * SUB, SUB) for jc in range(2)]
        limits = jnp.concatenate([counts[zb, pl.ds(start, SUB), :] for start in starts], axis=0)
        for s in range(CAP):
            cols = slice(s * BLOCK, (s + 1) * BLOCK)
            pre = mine[zb, :, cols] + theirs[zb, :, cols].astype(F32) + bias[pl.ds(tab[b, s], 1), :]
            rank = tab[b, 8 + s].astype(F32)
            out[zb, :, cols] = jnp.where(rank < limits, jnp.maximum(pre, 0.0), 0.0).astype(BF16)


def spread_kernel(pos, tab, lat0, lat1, out):
    zh, x, _, _, c = bits(pos)
    out[...] = jnp.zeros_like(out)
    b = zh * 4 + x
    for s in range(CAP):
        @pl.when(tab[b, 8 + s] < ACTIVE)
        def _():
            start = pl.multiple_of(tab[b, s] * BLOCK, BLOCK)
            for h, lat in enumerate((lat0, lat1)):
                for jc in range(2):
                    row = pl.multiple_of(h * 64 + (c ^ jc) * SUB, SUB)
                    value = lat[zh, jc * SUB : (jc + 1) * SUB, s * BLOCK : (s + 1) * BLOCK]
                    out[pl.ds(row, SUB), pl.ds(start, BLOCK)] = value


def decode_kernel(pos, tab, after, l0, l1, l2, l3, weight, mine, theirs):
    _, x, y, zl, _ = bits(pos)
    for k, lat in enumerate((l0, l1, l2, l3)):
        xb = x ^ k
        for zb in range(2):
            b = zb * 4 + xb
            acc = jnp.zeros((2 * SUB, SLICE), F32)
            for p in range(CAP // 2):
                tiles = [
                    weight[:, pl.ds(pl.multiple_of(tab[b, 2 * p + e] * BLOCK, BLOCK), BLOCK)] for e in range(2)
                ]
                acc = acc + lax.dot_general(
                    lat[zb, :, 2 * p * BLOCK : (2 * p + 2) * BLOCK],
                    jnp.concatenate(tiles, axis=1),
                    (((1,), (1,)), ((), ())),
                    preferred_element_type=F32,
                )
            ky = (zb * 2 + xb // 2) ^ y
            kz = (xb & 1) ^ (zl // 2)
            mine[ky, kz] = acc[:SUB]
            theirs[ky, kz] = acc[SUB:].astype(BF16)


def join_kernel(mine, theirs, wide, s1, s2, s3):
    for k, out in enumerate((wide, s1, s2, s3)):
        out[...] = (mine[k] + theirs[k].astype(F32)).astype(out.dtype)


def fold_kernel(pos, a0, a1, a2, a3, b0, b1, b2, b3, wide, s1, s2, s3):
    _, _, _, zl, _ = bits(pos)
    chunks = [
        p0[...] + p1[...].astype(F32) + p2[...].astype(F32) + p3[...].astype(F32)
        for p0, p1, p2, p3 in ((a0, a1, a2, a3), (b0, b1, b2, b3))
    ]
    for k, out in enumerate((wide, s1, s2, s3)):
        even = (zl & 1) == (k & 1)
        out[...] = jnp.where(even, chunks[0][k // 2], chunks[1][k // 2]).astype(out.dtype)


def tables(active_blocks, lat_index):
    ids = lat_index * SHARD_BLOCKS + jnp.arange(SHARD_BLOCKS, dtype=jnp.int32)
    matches = active_blocks[:, :, None] == ids[None, None, :]
    places = jnp.arange(ACTIVE, dtype=jnp.int32)[None, :, None]
    rank = jnp.sum(jnp.where(matches, places, 0), axis=1)
    listed = jnp.any(matches, axis=1).astype(jnp.int32)
    block = jnp.arange(SHARD_BLOCKS, dtype=jnp.int32)
    before = (block[:, None] < block[None, :]).astype(jnp.int32)
    slot = jnp.sum(listed[:, :, None] * before[None], axis=1)
    chosen = (slot[:, :, None] == jnp.arange(8, dtype=jnp.int32)[None, None, :]) & (listed[:, :, None] > 0)
    index = jnp.sum(jnp.where(chosen, block[None, :, None], 0), axis=1)
    ranks = jnp.sum(jnp.where(chosen, rank[:, :, None] - ACTIVE, 0), axis=1) + ACTIVE
    return jnp.concatenate([index, ranks], axis=1)


def shards(residual, enc_weight, dec_weight, enc_bias, dec_bias, active_blocks, active_counts):
    zh, x, y, zl, c = (lax.axis_index(a) for a in ("zh", "x", "y", "zl", "c"))
    pos = jnp.stack([zh, x, y, zl, c]).astype(jnp.int32)
    tab = tables(active_blocks, (y * 4 + zl) * 2 + c)

    pairs = []
    for source in range(256):
        r, lat = divmod(source, 32)
        pairs.append((source, (lat // 4) * 32 + r * 4 + lat % 4))
    own = lax.ppermute(residual.T, ROWS + LAT, pairs)
    near = gather4(gather4(own[None], "zl"), "y")
    other = swap(near, "c", 1)

    counts = active_counts.astype(F32).reshape(1, BLOCK)
    wide, narrow, full, own = call(
        gram_kernel,
        (
            jax.ShapeDtypeStruct((SUB, WIDE), F32),
            jax.ShapeDtypeStruct((SUB, WIDE), BF16),
            jax.ShapeDtypeStruct((SLICE, TOKENS), BF16),
            jax.ShapeDtypeStruct((SUB, SLICE), BF16),
        ),
        (pos, near, other, counts),
        [SMEM, VMEM, VMEM, VMEM],
        flops=2 * SUB * TOKENS * SLICE,
        size=1500000,
    )
    by2, by1, by3 = (swap(narrow, "x", k) for k in (2, 1, 3))
    mine, narrow = call(
        gram_sum_kernel,
        (jax.ShapeDtypeStruct((SUB, WIDE), F32), jax.ShapeDtypeStruct((SUB, WIDE), BF16)),
        (wide, by1, by2, by3),
        [VMEM] * 4,
        size=600000,
    )
    theirs = lax.ppermute(narrow, ("zh", "zl"), [(i, 7 - i) for i in range(8)])
    white = call(
        white_kernel,
        jax.ShapeDtypeStruct((1, SUB, SLICE), BF16),
        (pos, mine, theirs, full, own),
        [SMEM] + [VMEM] * 4,
        flops=4 * SUB * TOKENS * SLICE,
        size=1500000,
    )
    counts = call(
        counts_kernel,
        jax.ShapeDtypeStruct((2, BLOCK, BLOCK), F32),
        (pos, mine, theirs),
        [SMEM, VMEM, VMEM],
        size=500000,
        scratch=[pltpu.VMEM((8, BLOCK), F32)],
    )

    white_near = gather4(gather4(white, "zl"), "y")
    white_other = swap(white_near, "c", 1)
    bias = enc_bias.reshape(SHARD_BLOCKS, BLOCK)
    piece = jax.ShapeDtypeStruct((2, 2 * SUB, CAP * BLOCK), BF16)
    chunks = range(2)
    sent, sums, lats, parts = [], [], [], []
    for h in chunks:
        sent.append(
            call(
                functools.partial(encode_kernel, h),
                (piece,) * 4,
                (pos, tab, sent[0][0] if h else white_near, white_near, white_other, enc_weight),
                [SMEM, SMEM, ANY, VMEM, VMEM, VMEM],
                flops=TOKENS * SLICE * CAP * BLOCK,
                size=4000000,
            )
        )
    arrived = [[swap(sent[h][k], "x", k) for k in (2, 1, 3)] for h in chunks]
    for h in chunks:
        sums.append(
            call(
                sum_kernel,
                (jax.ShapeDtypeStruct(piece.shape, F32), piece),
                (sums[0][1] if h else sent[1][1], sent[h][0], *arrived[h]),
                [ANY] + [VMEM] * 4,
                size=1400000,
            )
        )
    theirs = [swap(sums[h][1], "zh", 1) for h in chunks]
    for h in chunks:
        lats.append(
            call(
                functools.partial(latent_kernel, h),
                piece,
                (pos, tab, lats[0] if h else white_near, sums[h][0], theirs[h], bias, counts),
                [SMEM, SMEM, ANY, VMEM, VMEM, VMEM, VMEM],
                size=1000000,
            )
        )
    arrived = [[swap(lats[h], "x", k) for k in (2, 1, 3)] for h in chunks]
    wide_part = jax.ShapeDtypeStruct((4, 2, SUB, SLICE), F32)
    narrow_part = jax.ShapeDtypeStruct((4, 2, SUB, SLICE), BF16)
    quarter = jax.ShapeDtypeStruct((2, SUB, SLICE), BF16)
    for h in chunks:
        far, by1, by3 = arrived[h]
        mine, theirs = call(
            decode_kernel,
            (wide_part, narrow_part),
            (pos, tab, parts[0][0] if h else lats[1], lats[h], by1, far, by3, dec_weight.T),
            [SMEM, SMEM, ANY] + [VMEM] * 5,
            flops=TOKENS * SLICE * CAP * BLOCK,
            size=5000000,
        )
        p0, p1, p2, p3 = call(
            join_kernel,
            (jax.ShapeDtypeStruct((2, SUB, SLICE), F32), quarter, quarter, quarter),
            (mine, swap(theirs, "c", 1)),
            [VMEM] * 2,
            size=1500000,
        )
        q2, q1, q3 = swap(p2, "y", 2), swap(p1, "y", 1), swap(p3, "y", 3)
        parts.append((p0, q1, q2, q3))
    latents = call(
        spread_kernel,
        jax.ShapeDtypeStruct((BLOCK, SHARD_BLOCKS * BLOCK), BF16),
        (pos, tab, *lats),
        [SMEM, SMEM, VMEM, VMEM],
        size=1000000,
    )
    small = jax.ShapeDtypeStruct((SUB, SLICE), BF16)
    recon, s1, s2, s3 = call(
        fold_kernel,
        (jax.ShapeDtypeStruct((SUB, SLICE), F32), small, small, small),
        (pos, *parts[0], *parts[1]),
        [SMEM] + [VMEM] * 8,
        size=1000000,
    )
    r2, r1, r3 = swap(s2, "zl", 2), swap(s1, "zl", 1), swap(s3, "zl", 3)
    recon = recon + r1.astype(F32) + r2.astype(F32) + r3.astype(F32)
    recon = (recon + dec_bias).astype(BF16)
    return latents, recon


def solution(mesh):
    fine = Mesh(mesh.devices.reshape(tuple(SIZES.values())), tuple(SIZES))
    in_specs = (P(ROWS, LAT), P(ROWS, LAT), P(LAT, ROWS), P(LAT), P(ROWS), P(), P(ROWS))
    out_specs = (P(ROWS, LAT), P(LAT, ROWS))
    return jax.shard_map(shards, mesh=fine, in_specs=in_specs, out_specs=out_specs, check_vma=False)
```

```python
import functools

import jax
import jax.numpy as jnp
from jax import lax
from jax.experimental import pallas as pl
from jax.experimental.pallas import tpu as pltpu
from jax.sharding import Mesh
from jax.sharding import PartitionSpec as P


BLOCK = 128
CAP = 6
TOKENS = 1024
D = 4608
SHARD_BLOCKS = 16
ACTIVE = 96
SLICE = 576
SUB = 32
ROWS = ("zh", "x")
LAT = ("y", "zl", "c")
SIZES = {"zh": 2, "x": 4, "y": 4, "zl": 4, "c": 2}
BF16 = jnp.bfloat16
F32 = jnp.float32

VMEM = pl.BlockSpec(memory_space=pltpu.VMEM)
SMEM = pl.BlockSpec(memory_space=pltpu.SMEM)
ANY = pl.BlockSpec(memory_space=pl.ANY)


def swap(value, axis, k):
    return lax.ppermute(value, axis, [(i, i ^ k) for i in range(SIZES[axis])])


def gather4(value, axis):
    far, near, last = (swap(value, axis, k) for k in (2, 1, 3))
    return jnp.concatenate([value, near, far, last], axis=0)


def call(kernel, outs, operands, specs, flops=0, size=0, scratch=()):
    return pl.pallas_call(
        kernel,
        out_shape=outs,
        in_specs=specs,
        out_specs=jax.tree.map(lambda _: VMEM, outs),
        scratch_shapes=scratch,
        compiler_params=pltpu.CompilerParams(vmem_limit_bytes=GRANT),
        cost_estimate=pl.CostEstimate(flops=flops, bytes_accessed=size, transcendentals=0),
    )(*operands)


def bits(pos):
    return pos[0], pos[1], pos[2], pos[3], pos[4]


GRANT = 10 * 2**20
WIDE = TOKENS + BLOCK


def row_group(zh, y, zl, c):
    return (y * 4 + (zl ^ (3 * zh))) * 2 + c


def on_diagonal(group):
    shape = (SUB, TOKENS)
    row = lax.broadcasted_iota(jnp.int32, shape, 0)
    return lax.broadcasted_iota(jnp.int32, shape, 1) == row + group * SUB


def split3(value):
    high = value.astype(BF16).astype(F32)
    mid = (value - high).astype(BF16).astype(F32)
    return high, mid, (value - high - mid).astype(BF16).astype(F32)


def pack(counts, diagonal, energy):
    row = lax.broadcasted_iota(jnp.int32, (SUB, BLOCK), 0)
    extra = jnp.where(row < 8, counts, 0.0)
    for i, part in enumerate(split3(diagonal) + split3(energy)):
        extra = jnp.where(row == 8 + i, part, extra)
    return extra


def gram_kernel(pos, near, other, counts, wide, narrow, full, own):
    zh, x, y, zl, c = bits(pos)
    for jc, half in enumerate((near, other)):
        for jy in range(4):
            for jz in range(4):
                zs = zl ^ jz
                feature = pl.multiple_of(((zs & 1) * 2 + (c ^ jc)) * 144, 16)
                source = ((zs // 2) ^ (x & 1) ^ zh) * 4 + ((zh * 2 + x // 2 + x + 2 - (y ^ jy)) & 3)
                row = pl.multiple_of(source * BLOCK, BLOCK)
                full[pl.ds(feature, 144), pl.ds(row, BLOCK)] = half[jy * 4 + jz]
    group = row_group(zh, y, zl, c)
    rows = full[:, pl.ds(pl.multiple_of(group // 4 * BLOCK, BLOCK), BLOCK)].astype(F32).T.astype(BF16)
    mine = rows[0:SUB]
    for g in range(1, 4):
        mine = jnp.where(group % 4 == g, rows[g * SUB : (g + 1) * SUB], mine)
    own[...] = mine
    g = jnp.dot(mine, full[...], preferred_element_type=F32)
    mask = on_diagonal(group)
    diagonal = jnp.sum(jnp.where(mask, g, 0.0), axis=0, keepdims=True)
    diagonal = sum(diagonal[:, i * BLOCK : (i + 1) * BLOCK] for i in range(TOKENS // BLOCK))
    g = jnp.where(mask, 0.0, g)
    wide[:, :TOKENS] = g
    narrow[:, :TOKENS] = g.astype(BF16)
    spread = full[...].astype(F32)
    total = jnp.sum(jnp.sum(spread * spread, axis=0, keepdims=True), axis=1, keepdims=True)
    shape = (SUB, BLOCK)
    row = lax.broadcasted_iota(jnp.int32, shape, 0)
    spot = jnp.where(row == zh * 4 + x, jnp.broadcast_to(counts[...], shape), 0.0)
    extra = pack(spot, jnp.broadcast_to(diagonal, shape), jnp.broadcast_to(total, shape))
    wide[:, TOKENS:] = extra
    narrow[:, TOKENS:] = extra.astype(BF16)


def unpack(extra):
    return extra[8:9] + extra[9:10] + extra[10:11], extra[11:12] + extra[12:13] + extra[13:14]


def gram_sum_kernel(mine, by1, by2, by3, wide, narrow):
    g = mine[...] + by1[...].astype(F32) + by2[...].astype(F32) + by3[...].astype(F32)
    wide[...] = g
    narrow[:, :TOKENS] = g[:, :TOKENS].astype(BF16)
    extra = g[:, TOKENS:]
    shape = (SUB, BLOCK)
    diagonal, energy = (jnp.broadcast_to(v, shape) for v in unpack(extra))
    narrow[:, TOKENS:] = pack(extra, diagonal, energy).astype(BF16)


def white_kernel(pos, mine, theirs, full, own, out):
    zh, _, y, zl, c = bits(pos)
    g = mine[...] + theirs[...].astype(F32)
    diagonal, energy = unpack(g[:, TOKENS:])
    mean_sq = energy[:, 0:1] / (TOKENS * D)
    diagonal = jnp.broadcast_to(jnp.concatenate([diagonal] * (TOKENS // BLOCK), axis=1), (SUB, TOKENS))
    g = jnp.where(on_diagonal(row_group(zh, y, zl, c)), diagonal, g[:, :TOKENS])
    chat = g / (TOKENS * (mean_sq + 1e-05))
    high = chat.astype(BF16)
    low = (chat - high.astype(F32)).astype(BF16)
    both = jnp.concatenate([high, low], axis=0)
    term = lax.dot_general(both, full[...], (((1,), (1,)), ((), ())), preferred_element_type=F32)
    out[0] = (1.5 * own[...].astype(F32) - 0.5 * (term[:SUB] + term[SUB:])).astype(BF16)


def counts_kernel(pos, mine, theirs, out, tile):
    tile[...] = mine[0:8, TOKENS:] + theirs[0:16, TOKENS:].astype(F32)[0:8]
    for zb in range(2):
        row = tile[pl.ds(pos[1] + 4 * zb, 1), :]
        out[zb] = jnp.broadcast_to(row, (BLOCK, BLOCK)).T


def encode_kernel(p, pos, tab, after, near, other, weight, o0, o1, o2, o3):
    zh, x, y, zl, _ = bits(pos)
    for k, out in ((2, o2), (1, o1), (3, o3), (0, o0)):
        xb = x ^ k
        for zb in range(2):
            b = zb * 4 + xb
            jy = y ^ (zb * 2 + xb // 2)
            places = [jy * 4 + (zl ^ (3 * zh) ^ ((xb & 1) * 2 + q)) for q in range(2)]
            rows = jnp.concatenate([half[place] for half in (near, other) for place in places], axis=0)
            cols = [weight[:, pl.ds(pl.multiple_of(tab[b, 2 * p + e] * BLOCK, BLOCK), BLOCK)] for e in range(2)]
            part = jnp.dot(rows, jnp.concatenate(cols, axis=1), preferred_element_type=F32)
            out[zb] = part.astype(BF16)


def sum_kernel(after, p0, p1, p2, p3, wide, narrow):
    total = p0[...].astype(F32) + p1[...].astype(F32) + p2[...].astype(F32) + p3[...].astype(F32)
    wide[...] = total
    narrow[...] = total.astype(BF16)


def row_start(q, jc, c):
    return pl.multiple_of(q * 64 + (c ^ jc) * SUB, SUB)


def latent_kernel(p, pos, tab, after, mine, theirs, bias, counts, out):
    _, x, _, _, c = bits(pos)
    for zb in range(2):
        b = zb * 4 + x
        limits = jnp.concatenate(
            [counts[zb, pl.ds(row_start(q, jc, c), SUB), :] for jc in range(2) for q in range(2)], axis=0
        )
        for e in range(2):
            slot = 2 * p + e
            cols = slice(e * BLOCK, (e + 1) * BLOCK)
            pre = mine[zb, :, cols] + theirs[zb, :, cols].astype(F32) + bias[pl.ds(tab[b, slot], 1), :]
            rank = tab[b, 8 + slot].astype(F32)
            out[zb, :, cols] = jnp.where(rank < limits, jnp.maximum(pre, 0.0), 0.0).astype(BF16)


def spread_kernel(pos, tab, lat0, lat1, lat2, out):
    zh, x, _, _, c = bits(pos)
    out[...] = jnp.zeros_like(out)
    b = zh * 4 + x
    for slot in range(CAP):
        @pl.when(tab[b, 8 + slot] < ACTIVE)
        def _():
            start = pl.multiple_of(tab[b, slot] * BLOCK, BLOCK)
            lat = (lat0, lat1, lat2)[slot // 2]
            cols = slice(slot % 2 * BLOCK, (slot % 2 + 1) * BLOCK)
            for jc in range(2):
                for q in range(2):
                    piece = jc * 2 + q
                    out[pl.ds(row_start(q, jc, c), SUB), pl.ds(start, BLOCK)] = lat[
                        zh, piece * SUB : (piece + 1) * SUB, cols
                    ]


def decode_pair(p, tab, lat, zb, b, weight):
    tiles = [weight[:, pl.ds(pl.multiple_of(tab[b, 2 * p + e] * BLOCK, BLOCK), BLOCK)] for e in range(2)]
    return lax.dot_general(
        lat[zb], jnp.concatenate(tiles, axis=1), (((1,), (1,)), ((), ())), preferred_element_type=F32
    )


def decode_kernel(pos, tab, after, *refs):
    first, second, weight, out = refs[0:4], refs[4:8], refs[8], refs[9]
    x = pos[1]
    for k in range(4):
        for zb in range(2):
            b = zb * 4 + (x ^ k)
            out[k, zb] = decode_pair(0, tab, first[k], zb, b, weight) + decode_pair(1, tab, second[k], zb, b, weight)


def finish_kernel(pos, tab, total, l0, l1, l2, l3, weight, mine, theirs):
    _, x, _, _, _ = bits(pos)
    for k, lat in enumerate((l0, l1, l2, l3)):
        xb = x ^ k
        for zb in range(2):
            acc = total[k, zb] + decode_pair(2, tab, lat, zb, zb * 4 + xb, weight)
            ky = zb * 2 + xb // 2
            for q in range(2):
                kz = (xb & 1) * 2 + q
                mine[ky, kz] = acc[q * SUB : (q + 1) * SUB]
                theirs[ky, kz] = acc[64 + q * SUB : 64 + (q + 1) * SUB].astype(BF16)


def join_kernel(mine, theirs, out):
    out[...] = (mine[...] + theirs[...].astype(F32)).astype(BF16)


def total_kernel(parts, bias, out):
    total = parts[0].astype(F32)
    for i in range(1, 16):
        total = total + parts[i].astype(F32)
    out[...] = (total + bias[...]).astype(BF16)


def tables(active_blocks, lat_index):
    ids = lat_index * SHARD_BLOCKS + jnp.arange(SHARD_BLOCKS, dtype=jnp.int32)
    matches = active_blocks[:, :, None] == ids[None, None, :]
    places = jnp.arange(ACTIVE, dtype=jnp.int32)[None, :, None]
    rank = jnp.sum(jnp.where(matches, places, 0), axis=1)
    listed = jnp.any(matches, axis=1).astype(jnp.int32)
    block = jnp.arange(SHARD_BLOCKS, dtype=jnp.int32)
    before = (block[:, None] < block[None, :]).astype(jnp.int32)
    slot = jnp.sum(listed[:, :, None] * before[None], axis=1)
    chosen = (slot[:, :, None] == jnp.arange(8, dtype=jnp.int32)[None, None, :]) & (listed[:, :, None] > 0)
    index = jnp.sum(jnp.where(chosen, block[None, :, None], 0), axis=1)
    ranks = jnp.sum(jnp.where(chosen, rank[:, :, None] - ACTIVE, 0), axis=1) + ACTIVE
    return jnp.concatenate([index, ranks], axis=1)


def shards(residual, enc_weight, dec_weight, enc_bias, dec_bias, active_blocks, active_counts):
    zh, x, y, zl, c = (lax.axis_index(a) for a in ("zh", "x", "y", "zl", "c"))
    pos = jnp.stack([zh, x, y, zl, c]).astype(jnp.int32)
    tab = tables(active_blocks, (y * 4 + zl) * 2 + c)

    pairs = []
    for source in range(256):
        r, lat = divmod(source, 32)
        half, xs = divmod(r, 4)
        ys, zs, core = lat // 8, lat // 2 % 4, lat % 2
        zh_to, x_to = divmod(lat // 4, 4)
        y_to, z_to = (ys + x_to - xs + 2) % 4, zs ^ (2 * (zh_to ^ half))
        pairs.append((source, (lat // 4) * 32 + y_to * 8 + z_to * 2 + core))
    own = lax.ppermute(residual.T, ROWS + LAT, pairs)
    near = gather4(gather4(own[None], "zl"), "y")
    other = swap(near, "c", 1)

    counts = active_counts.astype(F32).reshape(1, BLOCK)
    wide, narrow, full, own = call(
        gram_kernel,
        (
            jax.ShapeDtypeStruct((SUB, WIDE), F32),
            jax.ShapeDtypeStruct((SUB, WIDE), BF16),
            jax.ShapeDtypeStruct((SLICE, TOKENS), BF16),
            jax.ShapeDtypeStruct((SUB, SLICE), BF16),
        ),
        (pos, near, other, counts),
        [SMEM, VMEM, VMEM, VMEM],
        flops=2 * SUB * TOKENS * SLICE,
        size=1500000,
    )
    by2, by1, by3 = (swap(narrow, "x", k) for k in (2, 1, 3))
    mine, narrow = call(
        gram_sum_kernel,
        (jax.ShapeDtypeStruct((SUB, WIDE), F32), jax.ShapeDtypeStruct((SUB, WIDE), BF16)),
        (wide, by1, by2, by3),
        [VMEM] * 4,
        size=600000,
    )
    theirs = lax.ppermute(narrow, ("zh", "zl"), [(i, 7 - i) for i in range(8)])
    white = call(
        white_kernel,
        jax.ShapeDtypeStruct((1, SUB, SLICE), BF16),
        (pos, mine, theirs, full, own),
        [SMEM] + [VMEM] * 4,
        flops=4 * SUB * TOKENS * SLICE,
        size=1500000,
    )
    counts = call(
        counts_kernel,
        jax.ShapeDtypeStruct((2, BLOCK, BLOCK), F32),
        (pos, mine, theirs),
        [SMEM, VMEM, VMEM],
        size=500000,
        scratch=[pltpu.VMEM((8, BLOCK), F32)],
    )

    white_near = gather4(gather4(white, "zl"), "y")
    white_other = swap(white_near, "c", 1)
    bias = enc_bias.reshape(SHARD_BLOCKS, BLOCK)
    piece = jax.ShapeDtypeStruct((2, BLOCK, 2 * BLOCK), BF16)
    chunks = range(CAP // 2)
    sent, sums, lats = [], [], []
    for p in chunks:
        sent.append(
            call(
                functools.partial(encode_kernel, p),
                (piece,) * 4,
                (pos, tab, sent[-1][0] if p else white_near, white_near, white_other, enc_weight),
                [SMEM, SMEM, ANY, VMEM, VMEM, VMEM],
                flops=TOKENS * SLICE * 4 * BLOCK,
                size=3000000,
            )
        )
    arrived = [[swap(sent[p][k], "x", k) for k in (2, 1, 3)] for p in chunks]
    for p in chunks:
        sums.append(
            call(
                sum_kernel,
                (jax.ShapeDtypeStruct(piece.shape, F32), piece),
                (sums[-1][1] if p else sent[-1][0], sent[p][0], *arrived[p]),
                [ANY] + [VMEM] * 4,
                size=900000,
            )
        )
    theirs = [swap(sums[p][1], "zh", 1) for p in chunks]
    for p in chunks:
        lats.append(
            call(
                functools.partial(latent_kernel, p),
                piece,
                (pos, tab, lats[-1] if p else white_near, sums[p][0], theirs[p], bias, counts),
                [SMEM, SMEM, ANY, VMEM, VMEM, VMEM, VMEM],
                size=700000,
            )
        )
    arrived = []
    for p in chunks:
        by2, by1, by3 = (swap(lats[p], "x", k) for k in (2, 1, 3))
        arrived.append((lats[p], by1, by2, by3))
    dec_weight = dec_weight.T
    total = call(
        decode_kernel,
        jax.ShapeDtypeStruct((4, 2, BLOCK, SLICE), F32),
        (pos, tab, lats[-1], *arrived[0], *arrived[1], dec_weight),
        [SMEM, SMEM, ANY] + [VMEM] * 9,
        flops=TOKENS * SLICE * 8 * BLOCK,
        size=5000000,
    )
    part = (4, 4, SUB, SLICE)
    mine, theirs = call(
        finish_kernel,
        (jax.ShapeDtypeStruct(part, F32), jax.ShapeDtypeStruct(part, BF16)),
        (pos, tab, total, *arrived[2], dec_weight),
        [SMEM, SMEM] + [VMEM] * 6,
        flops=TOKENS * SLICE * 4 * BLOCK,
        size=5000000,
    )
    latents = call(
        spread_kernel,
        jax.ShapeDtypeStruct((BLOCK, SHARD_BLOCKS * BLOCK), BF16),
        (pos, tab, *lats),
        [SMEM, SMEM] + [VMEM] * 3,
        size=1000000,
    )
    joined = call(
        join_kernel, jax.ShapeDtypeStruct(part, BF16), (mine, swap(theirs, "c", 1)), [VMEM] * 2, size=4000000
    ).reshape(16, SUB, SLICE)
    recon = call(
        total_kernel,
        jax.ShapeDtypeStruct((SUB, SLICE), BF16),
        (lax.all_to_all(joined, ("y", "zl"), 0, 0, tiled=True), dec_bias.reshape(1, SLICE)),
        [VMEM] * 2,
        size=600000,
    )
    return latents, recon


def solution(mesh):
    fine = Mesh(mesh.devices.reshape(tuple(SIZES.values())), tuple(SIZES))
    in_specs = (P(ROWS, LAT), P(ROWS, LAT), P(LAT, ROWS), P(LAT), P(ROWS), P(), P(ROWS))
    out_specs = (P(ROWS, LAT), P(LAT, ROWS))
    return jax.shard_map(shards, mesh=fine, in_specs=in_specs, out_specs=out_specs, check_vma=False)
```

```python
import functools

import jax
import jax.numpy as jnp
from jax import lax
from jax.experimental import pallas as pl
from jax.experimental.pallas import tpu as pltpu
from jax.sharding import Mesh
from jax.sharding import PartitionSpec as P


BLOCK = 128
CAP = 6
TOKENS = 1024
D = 4608
SHARD_BLOCKS = 16
ACTIVE = 96
SLICE = 576
SUB = 32
ROWS = ("zh", "x")
LAT = ("y", "zl", "c")
SIZES = {"zh": 2, "x": 4, "y": 4, "zl": 4, "c": 2}
BF16 = jnp.bfloat16
F32 = jnp.float32

VMEM = pl.BlockSpec(memory_space=pltpu.VMEM)
SMEM = pl.BlockSpec(memory_space=pltpu.SMEM)
ANY = pl.BlockSpec(memory_space=pl.ANY)


def swap(value, axis, k):
    return lax.ppermute(value, axis, [(i, i ^ k) for i in range(SIZES[axis])])


def gather4(value, axis):
    far, near, last = (swap(value, axis, k) for k in (2, 1, 3))
    return jnp.concatenate([value, near, far, last], axis=0)


def call(kernel, outs, operands, specs, flops=0, size=0, scratch=()):
    return pl.pallas_call(
        kernel,
        out_shape=outs,
        in_specs=specs,
        out_specs=jax.tree.map(lambda _: VMEM, outs),
        scratch_shapes=scratch,
        compiler_params=pltpu.CompilerParams(vmem_limit_bytes=GRANT),
        cost_estimate=pl.CostEstimate(flops=flops, bytes_accessed=size, transcendentals=0),
    )(*operands)


def bits(pos):
    return pos[0], pos[1], pos[2], pos[3], pos[4]


GRANT = 10 * 2**20
WIDE = TOKENS + BLOCK


def row_group(zh, y, zl, c):
    return (y * 4 + (zl ^ (3 * zh))) * 2 + c


def on_diagonal(group):
    shape = (SUB, TOKENS)
    row = lax.broadcasted_iota(jnp.int32, shape, 0)
    return lax.broadcasted_iota(jnp.int32, shape, 1) == row + group * SUB


def split3(value):
    high = value.astype(BF16).astype(F32)
    mid = (value - high).astype(BF16).astype(F32)
    return high, mid, (value - high - mid).astype(BF16).astype(F32)


def pack(counts, diagonal, energy):
    row = lax.broadcasted_iota(jnp.int32, (SUB, BLOCK), 0)
    extra = jnp.where(row < 8, counts, 0.0)
    for i, part in enumerate(split3(diagonal) + split3(energy)):
        extra = jnp.where(row == 8 + i, part, extra)
    return extra


def gram_kernel(pos, near, other, counts, wide, narrow, full, own):
    zh, x, y, zl, c = bits(pos)
    for jc, half in enumerate((near, other)):
        for jy in range(4):
            for jz in range(4):
                zs = zl ^ jz
                feature = pl.multiple_of(((zs & 1) * 2 + (c ^ jc)) * 144, 16)
                source = ((zs // 2) ^ (x & 1) ^ zh) * 4 + ((zh * 2 + x // 2 + x + 2 - (y ^ jy)) & 3)
                row = pl.multiple_of(source * BLOCK, BLOCK)
                full[pl.ds(feature, 144), pl.ds(row, BLOCK)] = half[jy * 4 + jz]
    group = row_group(zh, y, zl, c)
    rows = full[:, pl.ds(pl.multiple_of(group // 4 * BLOCK, BLOCK), BLOCK)].astype(F32).T.astype(BF16)
    mine = rows[0:SUB]
    for g in range(1, 4):
        mine = jnp.where(group % 4 == g, rows[g * SUB : (g + 1) * SUB], mine)
    own[...] = mine
    g = jnp.dot(mine, full[...], preferred_element_type=F32)
    mask = on_diagonal(group)
    diagonal = jnp.sum(jnp.where(mask, g, 0.0), axis=0, keepdims=True)
    diagonal = sum(diagonal[:, i * BLOCK : (i + 1) * BLOCK] for i in range(TOKENS // BLOCK))
    g = jnp.where(mask, 0.0, g)
    wide[:, :TOKENS] = g
    narrow[:, :TOKENS] = g.astype(BF16)
    spread = full[...].astype(F32)
    total = jnp.sum(jnp.sum(spread * spread, axis=0, keepdims=True), axis=1, keepdims=True)
    shape = (SUB, BLOCK)
    row = lax.broadcasted_iota(jnp.int32, shape, 0)
    spot = jnp.where(row == zh * 4 + x, jnp.broadcast_to(counts[...], shape), 0.0)
    extra = pack(spot, jnp.broadcast_to(diagonal, shape), jnp.broadcast_to(total, shape))
    wide[:, TOKENS:] = extra
    narrow[:, TOKENS:] = extra.astype(BF16)


def unpack(extra):
    return extra[8:9] + extra[9:10] + extra[10:11], extra[11:12] + extra[12:13] + extra[13:14]


def gram_sum_kernel(mine, by1, by2, by3, wide, narrow):
    g = mine[...] + by1[...].astype(F32) + by2[...].astype(F32) + by3[...].astype(F32)
    wide[...] = g
    narrow[:, :TOKENS] = g[:, :TOKENS].astype(BF16)
    extra = g[:, TOKENS:]
    shape = (SUB, BLOCK)
    diagonal, energy = (jnp.broadcast_to(v, shape) for v in unpack(extra))
    narrow[:, TOKENS:] = pack(extra, diagonal, energy).astype(BF16)


def white_kernel(pos, mine, theirs, full, own, out):
    zh, _, y, zl, c = bits(pos)
    g = mine[...] + theirs[...].astype(F32)
    diagonal, energy = unpack(g[:, TOKENS:])
    mean_sq = energy[:, 0:1] / (TOKENS * D)
    diagonal = jnp.broadcast_to(jnp.concatenate([diagonal] * (TOKENS // BLOCK), axis=1), (SUB, TOKENS))
    g = jnp.where(on_diagonal(row_group(zh, y, zl, c)), diagonal, g[:, :TOKENS])
    chat = g / (TOKENS * (mean_sq + 1e-05))
    high = chat.astype(BF16)
    low = (chat - high.astype(F32)).astype(BF16)
    both = jnp.concatenate([high, low], axis=0)
    term = lax.dot_general(both, full[...], (((1,), (1,)), ((), ())), preferred_element_type=F32)
    out[0] = (1.5 * own[...].astype(F32) - 0.5 * (term[:SUB] + term[SUB:])).astype(BF16)


def counts_kernel(pos, mine, theirs, out, tile):
    tile[...] = mine[0:8, TOKENS:] + theirs[0:16, TOKENS:].astype(F32)[0:8]
    for zb in range(2):
        row = tile[pl.ds(pos[1] + 4 * zb, 1), :]
        out[zb] = jnp.broadcast_to(row, (BLOCK, BLOCK)).T


def encode_kernel(p, pos, tab, after, near, other, weight, o0, o1, o2, o3):
    zh, x, y, zl, _ = bits(pos)
    for k, out in ((2, o2), (1, o1), (3, o3), (0, o0)):
        xb = x ^ k
        for zb in range(2):
            b = zb * 4 + xb
            jy = y ^ (zb * 2 + xb // 2)
            places = [jy * 4 + (zl ^ (3 * zh) ^ ((xb & 1) * 2 + q)) for q in range(2)]
            rows = jnp.concatenate([half[place] for half in (near, other) for place in places], axis=0)
            cols = [weight[:, pl.ds(pl.multiple_of(tab[b, 2 * p + e] * BLOCK, BLOCK), BLOCK)] for e in range(2)]
            part = jnp.dot(rows, jnp.concatenate(cols, axis=1), preferred_element_type=F32)
            out[zb] = part.astype(BF16)


def sum_kernel(after, p0, p1, p2, p3, wide, narrow):
    total = p0[...].astype(F32) + p1[...].astype(F32) + p2[...].astype(F32) + p3[...].astype(F32)
    wide[...] = total
    narrow[...] = total.astype(BF16)


def row_start(q, jc, c):
    return pl.multiple_of(q * 64 + (c ^ jc) * SUB, SUB)


def latent_kernel(p, pos, tab, after, mine, theirs, bias, counts, out):
    _, x, _, _, c = bits(pos)
    for zb in range(2):
        b = zb * 4 + x
        limits = jnp.concatenate(
            [counts[zb, pl.ds(row_start(q, jc, c), SUB), :] for jc in range(2) for q in range(2)], axis=0
        )
        for e in range(2):
            slot = 2 * p + e
            cols = slice(e * BLOCK, (e + 1) * BLOCK)
            pre = mine[zb, :, cols] + theirs[zb, :, cols].astype(F32) + bias[pl.ds(tab[b, slot], 1), :]
            rank = tab[b, 8 + slot].astype(F32)
            out[zb, :, cols] = jnp.where(rank < limits, jnp.maximum(pre, 0.0), 0.0).astype(BF16)


def spread_kernel(pos, tab, lat0, lat1, lat2, out):
    zh, x, _, _, c = bits(pos)
    out[...] = jnp.zeros_like(out)
    b = zh * 4 + x
    for slot in range(CAP):
        @pl.when(tab[b, 8 + slot] < ACTIVE)
        def _():
            start = pl.multiple_of(tab[b, slot] * BLOCK, BLOCK)
            lat = (lat0, lat1, lat2)[slot // 2]
            cols = slice(slot % 2 * BLOCK, (slot % 2 + 1) * BLOCK)
            for jc in range(2):
                for q in range(2):
                    piece = jc * 2 + q
                    out[pl.ds(row_start(q, jc, c), SUB), pl.ds(start, BLOCK)] = lat[
                        zh, piece * SUB : (piece + 1) * SUB, cols
                    ]


def decode_pair(p, tab, lat, zb, b, weight):
    tiles = [weight[:, pl.ds(pl.multiple_of(tab[b, 2 * p + e] * BLOCK, BLOCK), BLOCK)] for e in range(2)]
    return lax.dot_general(
        lat[zb], jnp.concatenate(tiles, axis=1), (((1,), (1,)), ((), ())), preferred_element_type=F32
    )


def decode_kernel(pos, tab, after, *refs):
    first, second, weight, out = refs[0:4], refs[4:8], refs[8], refs[9]
    x = pos[1]
    for k in range(4):
        for zb in range(2):
            b = zb * 4 + (x ^ k)
            out[k, zb] = decode_pair(0, tab, first[k], zb, b, weight) + decode_pair(1, tab, second[k], zb, b, weight)


def finish_kernel(pos, tab, total, l0, l1, l2, l3, weight, mine, theirs):
    _, x, y, zl, _ = bits(pos)
    for k, lat in enumerate((l0, l1, l2, l3)):
        xb = x ^ k
        for zb in range(2):
            acc = total[k, zb] + decode_pair(2, tab, lat, zb, zb * 4 + xb, weight)
            ky = (zb * 2 + xb // 2) ^ y
            for q in range(2):
                kz = ((xb & 1) * 2 + q) ^ zl
                mine[ky, kz] = acc[q * SUB : (q + 1) * SUB]
                theirs[ky, kz] = acc[64 + q * SUB : 64 + (q + 1) * SUB].astype(BF16)


def join_kernel(mine, theirs, wide, s1, s2, s3):
    for k, out in enumerate((wide, s1, s2, s3)):
        out[...] = (mine[k] + theirs[k].astype(F32)).astype(out.dtype)


def fold_kernel(p0, p1, p2, p3, wide, s1, s2, s3):
    for k, out in enumerate((wide, s1, s2, s3)):
        total = p0[k] + p1[k].astype(F32) + p2[k].astype(F32) + p3[k].astype(F32)
        out[...] = total.astype(out.dtype)


def tables(active_blocks, lat_index):
    ids = lat_index * SHARD_BLOCKS + jnp.arange(SHARD_BLOCKS, dtype=jnp.int32)
    matches = active_blocks[:, :, None] == ids[None, None, :]
    places = jnp.arange(ACTIVE, dtype=jnp.int32)[None, :, None]
    rank = jnp.sum(jnp.where(matches, places, 0), axis=1)
    listed = jnp.any(matches, axis=1).astype(jnp.int32)
    block = jnp.arange(SHARD_BLOCKS, dtype=jnp.int32)
    before = (block[:, None] < block[None, :]).astype(jnp.int32)
    slot = jnp.sum(listed[:, :, None] * before[None], axis=1)
    chosen = (slot[:, :, None] == jnp.arange(8, dtype=jnp.int32)[None, None, :]) & (listed[:, :, None] > 0)
    index = jnp.sum(jnp.where(chosen, block[None, :, None], 0), axis=1)
    ranks = jnp.sum(jnp.where(chosen, rank[:, :, None] - ACTIVE, 0), axis=1) + ACTIVE
    return jnp.concatenate([index, ranks], axis=1)


def shards(residual, enc_weight, dec_weight, enc_bias, dec_bias, active_blocks, active_counts):
    zh, x, y, zl, c = (lax.axis_index(a) for a in ("zh", "x", "y", "zl", "c"))
    pos = jnp.stack([zh, x, y, zl, c]).astype(jnp.int32)
    tab = tables(active_blocks, (y * 4 + zl) * 2 + c)

    pairs = []
    for source in range(256):
        r, lat = divmod(source, 32)
        half, xs = divmod(r, 4)
        ys, zs, core = lat // 8, lat // 2 % 4, lat % 2
        zh_to, x_to = divmod(lat // 4, 4)
        y_to, z_to = (ys + x_to - xs + 2) % 4, zs ^ (2 * (zh_to ^ half))
        pairs.append((source, (lat // 4) * 32 + y_to * 8 + z_to * 2 + core))
    own = lax.ppermute(residual.T, ROWS + LAT, pairs)
    near = gather4(gather4(own[None], "zl"), "y")
    other = swap(near, "c", 1)

    counts = active_counts.astype(F32).reshape(1, BLOCK)
    wide, narrow, full, own = call(
        gram_kernel,
        (
            jax.ShapeDtypeStruct((SUB, WIDE), F32),
            jax.ShapeDtypeStruct((SUB, WIDE), BF16),
            jax.ShapeDtypeStruct((SLICE, TOKENS), BF16),
            jax.ShapeDtypeStruct((SUB, SLICE), BF16),
        ),
        (pos, near, other, counts),
        [SMEM, VMEM, VMEM, VMEM],
        flops=2 * SUB * TOKENS * SLICE,
        size=1500000,
    )
    by2, by1, by3 = (swap(narrow, "x", k) for k in (2, 1, 3))
    mine, narrow = call(
        gram_sum_kernel,
        (jax.ShapeDtypeStruct((SUB, WIDE), F32), jax.ShapeDtypeStruct((SUB, WIDE), BF16)),
        (wide, by1, by2, by3),
        [VMEM] * 4,
        size=600000,
    )
    theirs = lax.ppermute(narrow, ("zh", "zl"), [(i, 7 - i) for i in range(8)])
    white = call(
        white_kernel,
        jax.ShapeDtypeStruct((1, SUB, SLICE), BF16),
        (pos, mine, theirs, full, own),
        [SMEM] + [VMEM] * 4,
        flops=4 * SUB * TOKENS * SLICE,
        size=1500000,
    )
    counts = call(
        counts_kernel,
        jax.ShapeDtypeStruct((2, BLOCK, BLOCK), F32),
        (pos, mine, theirs),
        [SMEM, VMEM, VMEM],
        size=500000,
        scratch=[pltpu.VMEM((8, BLOCK), F32)],
    )

    white_near = gather4(gather4(white, "zl"), "y")
    white_other = swap(white_near, "c", 1)
    bias = enc_bias.reshape(SHARD_BLOCKS, BLOCK)
    piece = jax.ShapeDtypeStruct((2, BLOCK, 2 * BLOCK), BF16)
    chunks = range(CAP // 2)
    sent, sums, lats = [], [], []
    for p in chunks:
        sent.append(
            call(
                functools.partial(encode_kernel, p),
                (piece,) * 4,
                (pos, tab, sent[-1][0] if p else white_near, white_near, white_other, enc_weight),
                [SMEM, SMEM, ANY, VMEM, VMEM, VMEM],
                flops=TOKENS * SLICE * 4 * BLOCK,
                size=3000000,
            )
        )
    arrived = [[swap(sent[p][k], "x", k) for k in (2, 1, 3)] for p in chunks]
    for p in chunks:
        sums.append(
            call(
                sum_kernel,
                (jax.ShapeDtypeStruct(piece.shape, F32), piece),
                (sums[-1][1] if p else sent[-1][0], sent[p][0], *arrived[p]),
                [ANY] + [VMEM] * 4,
                size=900000,
            )
        )
    theirs = [swap(sums[p][1], "zh", 1) for p in chunks]
    for p in chunks:
        lats.append(
            call(
                functools.partial(latent_kernel, p),
                piece,
                (pos, tab, lats[-1] if p else white_near, sums[p][0], theirs[p], bias, counts),
                [SMEM, SMEM, ANY, VMEM, VMEM, VMEM, VMEM],
                size=700000,
            )
        )
    arrived = []
    for p in chunks:
        by2, by1, by3 = (swap(lats[p], "x", k) for k in (2, 1, 3))
        arrived.append((lats[p], by1, by2, by3))
    dec_weight = dec_weight.T
    total = call(
        decode_kernel,
        jax.ShapeDtypeStruct((4, 2, BLOCK, SLICE), F32),
        (pos, tab, lats[-1], *arrived[0], *arrived[1], dec_weight),
        [SMEM, SMEM, ANY] + [VMEM] * 9,
        flops=TOKENS * SLICE * 8 * BLOCK,
        size=5000000,
    )
    part = (4, 4, SUB, SLICE)
    mine, theirs = call(
        finish_kernel,
        (jax.ShapeDtypeStruct(part, F32), jax.ShapeDtypeStruct(part, BF16)),
        (pos, tab, total, *arrived[2], dec_weight),
        [SMEM, SMEM] + [VMEM] * 6,
        flops=TOKENS * SLICE * 4 * BLOCK,
        size=5000000,
    )
    latents = call(
        spread_kernel,
        jax.ShapeDtypeStruct((BLOCK, SHARD_BLOCKS * BLOCK), BF16),
        (pos, tab, *lats),
        [SMEM, SMEM] + [VMEM] * 3,
        size=1000000,
    )
    quarter = jax.ShapeDtypeStruct(part[1:], BF16)
    p0, p1, p2, p3 = call(
        join_kernel,
        (jax.ShapeDtypeStruct(part[1:], F32), quarter, quarter, quarter),
        (mine, swap(theirs, "c", 1)),
        [VMEM] * 2,
        size=3000000,
    )
    q2, q1, q3 = swap(p2, "y", 2), swap(p1, "y", 1), swap(p3, "y", 3)
    small = jax.ShapeDtypeStruct((SUB, SLICE), BF16)
    recon, s1, s2, s3 = call(
        fold_kernel,
        (jax.ShapeDtypeStruct((SUB, SLICE), F32), small, small, small),
        (p0, q1, q2, q3),
        [VMEM] * 4,
        size=1000000,
    )
    r2, r1, r3 = swap(s2, "zl", 2), swap(s1, "zl", 1), swap(s3, "zl", 3)
    recon = recon + r1.astype(F32) + r2.astype(F32) + r3.astype(F32)
    recon = (recon + dec_bias).astype(BF16)
    return latents, recon


def solution(mesh):
    fine = Mesh(mesh.devices.reshape(tuple(SIZES.values())), tuple(SIZES))
    in_specs = (P(ROWS, LAT), P(ROWS, LAT), P(LAT, ROWS), P(LAT), P(ROWS), P(), P(ROWS))
    out_specs = (P(ROWS, LAT), P(LAT, ROWS))
    return jax.shard_map(shards, mesh=fine, in_specs=in_specs, out_specs=out_specs, check_vma=False)
```
